512 devices in a mesh: space: 16 (over y, x), mom: 32 (over z, core).
Axes of the slice: x: 4, y: 4, z: 16, core: 2. Of those that a mesh axis runs over, the one named last changes fastest.
Arguments:
- distribution: float32 [3, 512, 8, 96, 128], P(None, 'space', None, 'mom'), as said below
- cutoff: int32 [512, 8], P('space'), may hold values from 48 to 96
- phonon_shift: int32 [4], replicated, may hold values from 1 to 8
- phonon_rates: float32 [2, 4], replicated, may hold values from 0.02 to 0.12
Outputs:
- sectioned: float32 [3, 512, 8, 96, 128], P(None, 'space', None, 'mom')
- density: float32 [4096], P(('space', 'mom'))
The draws below stay inside these ranges and needn't reach their ends.
Inputs may be any that keep to these rules, and one draw needn't show every extreme that they name: `distribution`: the cell means (component 0) are positive.
All inputs are finite; a program needn't handle non-finite values.
Results may differ from the reference program's by a relative error of at most 0.0003.
Values sent between devices are 32-bit elements; how exact they have to be, the bound alone decides.
A program may use at most 64 MiB of HBM per device.

```python
import math
import jax
import jax.numpy as jnp
from jax import lax

NY = 8
NE = 96
NPOL = 16
NAZ = 8
NPHON = 4
NDIR = 128
NX = 512


def draw_distribution(key, part):
    keys = jax.random.split(key, 2)
    energy = jnp.arange(NE, dtype=jnp.float32)
    profile = jnp.exp(-1.2 * energy / NE)[None, None, :, None]
    rough = jax.random.uniform(keys[0], (NX, NY, NE, NDIR), jnp.float32, 0.2, 1.5)
    level = profile * rough
    slopes = 0.45 * level[None] * jax.random.normal(keys[1], (2, NX, NY, NE, NDIR), jnp.float32)
    return jnp.concatenate([level[None], slopes], axis=0)


def place_ends(entries, key, low, high):
    dims = entries.shape
    index_at = [jax.random.randint(jax.random.fold_in(key, axis), (), 0, dims[axis]) for axis in range(len(dims))]
    entries = entries.at[tuple(index_at)].set(low)
    longest = dims.index(max(dims))
    index_at[longest] = (index_at[longest] + 1) % dims[longest]
    return entries.at[tuple(index_at)].set(high)


def setup_inputs(seed: int = 0) -> dict:
    streams_of = jax.random.split(jax.random.key(seed), 5)
    return {
        "distribution": draw_distribution(jax.random.fold_in(streams_of[4], 71), 0),
        "cutoff": place_ends(jax.random.randint(streams_of[1], (NX, NY), NE // 2, NE + 1), jax.random.fold_in(streams_of[1], 1), NE // 2, NE).astype(jnp.int32),
        "phonon_shift": place_ends(jax.random.randint(streams_of[2], (NPHON,), 1, 9), jax.random.fold_in(streams_of[2], 1), 1, 8).astype(jnp.int32),
        "phonon_rates": jnp.clip(jnp.exp(jax.random.uniform(streams_of[3], (2, NPHON), jnp.float32, math.log(0.02), math.log(0.12))), 0.02, 0.12),
    }


COURANT = 0.25
FLOOR = 0.1

def velocities(energy):
    flight_speed = jnp.sqrt((energy + 0.5) / NE)
    polar_index = jnp.arange(NPOL, dtype=jnp.float32)
    cos_polar = -1.0 + (2.0 * polar_index + 1.0) / NPOL
    azimuth = (jnp.arange(NAZ, dtype=jnp.float32) + 0.5) * (2.0 * math.pi / NAZ)
    along_x = jnp.repeat(cos_polar, NAZ)
    across_y = (jnp.sqrt(1.0 - cos_polar * cos_polar)[:, None] * jnp.cos(azimuth)[None, :]).reshape(NPOL * NAZ)
    return (COURANT * flight_speed * along_x, COURANT * flight_speed * across_y)

def transport(padded, vel_x, vel_y):
    level = padded[0]
    slope_x = padded[1]
    slope_y = padded[2]
    right_vel = jnp.maximum(vel_x, 0.0)
    left_vel = jnp.minimum(vel_x, 0.0)
    face_mean = right_vel * (level + slope_x)[:-1] + left_vel * (level - slope_x)[1:]
    face_cross = right_vel * slope_y[:-1] + left_vel * slope_y[1:]
    inner_level = level[1:-1]
    inner_x = slope_x[1:-1]
    inner_y = slope_y[1:-1]
    rate_level = -(face_mean[1:] - face_mean[:-1])
    rate_x = -3.0 * (face_mean[1:] + face_mean[:-1] - 2.0 * vel_x * inner_level)
    rate_y = -(face_cross[1:] - face_cross[:-1])
    widths = [(0, 0)] * inner_level.ndim
    widths[1] = (1, 1)
    pad_level = jnp.pad(inner_level, widths)
    pad_x = jnp.pad(inner_x, widths)
    pad_y = jnp.pad(inner_y, widths)
    up_vel = jnp.maximum(vel_y, 0.0)
    down_vel = jnp.minimum(vel_y, 0.0)
    edge_mean = up_vel * (pad_level + pad_y)[:, :-1] + down_vel * (pad_level - pad_y)[:, 1:]
    edge_cross = up_vel * pad_x[:, :-1] + down_vel * pad_x[:, 1:]
    rate_level = rate_level - (edge_mean[:, 1:] - edge_mean[:, :-1])
    rate_y = rate_y - 3.0 * (edge_mean[:, 1:] + edge_mean[:, :-1] - 2.0 * vel_y * inner_level)
    rate_x = rate_x - (edge_cross[:, 1:] - edge_cross[:, :-1])
    return jnp.stack([rate_level, rate_x, rate_y])

def kernel_parts(phonon_rates, phonon_shift):
    target = jnp.arange(NE, dtype=jnp.int32)[:, None]
    source = jnp.arange(NE, dtype=jnp.int32)[None, :]
    offsets = phonon_shift[:, None, None]
    absorb = (source[None] == target[None] - offsets).astype(jnp.float32)
    emitted = (source[None] == target[None] + offsets).astype(jnp.float32)
    matrix = lax.optimization_barrier(jnp.sum(phonon_rates[0][:, None, None] * absorb + phonon_rates[1][:, None, None] * emitted, axis=0))
    energy = jnp.arange(NE, dtype=jnp.int32)[None, :]
    upper = (energy + phonon_shift[:, None] < NE).astype(jnp.float32)
    lower = (energy - phonon_shift[:, None] >= 0).astype(jnp.float32)
    out_rate = lax.optimization_barrier(jnp.sum(phonon_rates[0][:, None] * upper + phonon_rates[1][:, None] * lower, axis=0))
    return (matrix, out_rate)

def limit(state):
    spread = jnp.abs(state[1]) + jnp.abs(state[2])
    scaling = jnp.minimum(1.0, jnp.maximum(state[0], 0.0) / jnp.maximum(spread, FLOOR))
    return jnp.stack([state[0], scaling * state[1], scaling * state[2]])

def reference(distribution, cutoff, phonon_shift, phonon_rates):
    levels = jnp.arange(NE, dtype=jnp.int32)
    mask = (levels[None, None, :] < cutoff[:, :, None]).astype(jnp.float32)
    masked = distribution * mask[None, :, :, :, None]
    moments = lax.optimization_barrier(jnp.mean(masked, axis=4))
    matrix, out_rate = kernel_parts(phonon_rates, phonon_shift)
    gain = jnp.einsum('dxye,fe->dxyf', moments, matrix, precision=lax.Precision.HIGHEST)

    def one_energy(index):
        block = lax.dynamic_index_in_dim(masked, index, 3, keepdims=False)
        vel_x, vel_y = velocities(index.astype(jnp.float32))
        padded = jnp.pad(block, ((0, 0), (1, 1), (0, 0), (0, 0)))
        tendency = transport(padded, vel_x, vel_y)
        gain_here = lax.dynamic_index_in_dim(gain, index, 3, keepdims=False)
        rate_here = lax.dynamic_index_in_dim(out_rate, index, 0, keepdims=False)
        collision = gain_here[..., None] - rate_here * block
        mask_here = lax.dynamic_index_in_dim(mask, index, 2, keepdims=False)
        return limit(mask_here[None, :, :, None] * (block + tendency + collision))
    stacked = lax.map(one_energy, levels)
    sectioned = jnp.moveaxis(stacked, 0, 3)
    density = lax.optimization_barrier(jnp.mean(sectioned[0], axis=(2, 3))).reshape(NX * NY)
    return (sectioned, density)
```

```python
import math

import jax
import jax.numpy as jnp
from jax import lax
from jax.sharding import PartitionSpec as P

NE = 96
NPOL = 16
NAZ = 8
NDIR = 128


COURANT = 0.25
FLOOR = 0.1


def padded_2(x, sides, width):
    for axis, dim in sides:
        count, length = (lax.axis_size(axis), x.shape[dim])
        up = [(i, (i + 1) % count) for i in range(count - 1)]
        down = [(j, i) for i, j in up]
        last = lax.slice_in_dim(x, length - width, length, axis=dim)
        leading = lax.slice_in_dim(x, 0, width, axis=dim)
        before = lax.ppermute(last, axis, up)
        after = lax.ppermute(leading, axis, down)
        x = jnp.concatenate([before, x, after], axis=dim)
    return x


def velocities(energy):
    flight_speed = jnp.sqrt((energy + 0.5) / NE)
    polar_index = jnp.arange(NPOL, dtype=jnp.float32)
    cos_polar = -1.0 + (2.0 * polar_index + 1.0) / NPOL
    azimuth = (jnp.arange(NAZ, dtype=jnp.float32) + 0.5) * (2.0 * math.pi / NAZ)
    along_x = jnp.repeat(cos_polar, NAZ)
    across_y = (jnp.sqrt(1.0 - cos_polar * cos_polar)[:, None] * jnp.cos(azimuth)[None, :]).reshape(
        NPOL * NAZ
    )
    return (COURANT * flight_speed * along_x, COURANT * flight_speed * across_y)


def transport(padded, vel_x, vel_y):
    level = padded[0]
    slope_x = padded[1]
    slope_y = padded[2]
    right_vel = jnp.maximum(vel_x, 0.0)
    left_vel = jnp.minimum(vel_x, 0.0)
    face_mean = right_vel * (level + slope_x)[:-1] + left_vel * (level - slope_x)[1:]
    face_cross = right_vel * slope_y[:-1] + left_vel * slope_y[1:]
    inner_level = level[1:-1]
    inner_x = slope_x[1:-1]
    inner_y = slope_y[1:-1]
    rate_level = -(face_mean[1:] - face_mean[:-1])
    rate_x = -3.0 * (face_mean[1:] + face_mean[:-1] - 2.0 * vel_x * inner_level)
    rate_y = -(face_cross[1:] - face_cross[:-1])
    widths = [(0, 0)] * inner_level.ndim
    widths[1] = (1, 1)
    pad_level = jnp.pad(inner_level, widths)
    pad_x = jnp.pad(inner_x, widths)
    pad_y = jnp.pad(inner_y, widths)
    up_vel = jnp.maximum(vel_y, 0.0)
    down_vel = jnp.minimum(vel_y, 0.0)
    edge_mean = up_vel * (pad_level + pad_y)[:, :-1] + down_vel * (pad_level - pad_y)[:, 1:]
    edge_cross = up_vel * pad_x[:, :-1] + down_vel * pad_x[:, 1:]
    rate_level = rate_level - (edge_mean[:, 1:] - edge_mean[:, :-1])
    rate_y = rate_y - 3.0 * (edge_mean[:, 1:] + edge_mean[:, :-1] - 2.0 * vel_y * inner_level)
    rate_x = rate_x - (edge_cross[:, 1:] - edge_cross[:, :-1])
    return jnp.stack([rate_level, rate_x, rate_y])


def kernel_parts(phonon_rates, phonon_shift):
    target = jnp.arange(NE, dtype=jnp.int32)[:, None]
    source = jnp.arange(NE, dtype=jnp.int32)[None, :]
    offsets = phonon_shift[:, None, None]
    absorb = (source[None] == target[None] - offsets).astype(jnp.float32)
    emitted = (source[None] == target[None] + offsets).astype(jnp.float32)
    matrix = jnp.sum(
        phonon_rates[0][:, None, None] * absorb + phonon_rates[1][:, None, None] * emitted, axis=0
    )
    energy = jnp.arange(NE, dtype=jnp.int32)[None, :]
    upper = (energy + phonon_shift[:, None] < NE).astype(jnp.float32)
    lower = (energy - phonon_shift[:, None] >= 0).astype(jnp.float32)
    out_rate = jnp.sum(phonon_rates[0][:, None] * upper + phonon_rates[1][:, None] * lower, axis=0)
    return (matrix, out_rate)


def limit(state):
    spread = jnp.abs(state[1]) + jnp.abs(state[2])
    scaling = jnp.minimum(1.0, jnp.maximum(state[0], 0.0) / jnp.maximum(spread, FLOOR))
    return jnp.stack([state[0], scaling * state[1], scaling * state[2]])


def on_device(distribution, cutoff, phonon_shift, phonon_rates):
    comps, slab_x, rows_y, local_e, dirs = distribution.shape
    cells = slab_x * rows_y
    first_energy = lax.axis_index("mom") * local_e
    levels = first_energy + jnp.arange(local_e, dtype=jnp.int32)
    mask = (levels[None, None, :] < cutoff[:, :, None]).astype(jnp.float32)
    masked = distribution * mask[None, :, :, :, None]
    vel_x, vel_y = velocities(levels.astype(jnp.float32)[:, None])
    padded = padded_2(masked, (("space", 1),), 1)
    tendency = transport(padded, vel_x, vel_y)
    matrix, out_rate = kernel_parts(phonon_rates, phonon_shift)
    angular = jnp.mean(masked, axis=4).reshape(comps, cells, local_e)
    block = lax.all_to_all(angular, "mom", split_axis=1, concat_axis=2, tiled=True)
    gain = jnp.einsum("dce,fe->dcf", block, matrix, precision=lax.Precision.HIGHEST)
    gain = lax.all_to_all(gain, "mom", split_axis=2, concat_axis=1, tiled=True).reshape(
        comps, slab_x, rows_y, local_e, 1
    )
    local_out = lax.dynamic_slice_in_dim(out_rate, first_energy, local_e)
    collision = gain - local_out[:, None] * masked
    sectioned = limit(mask[None, :, :, :, None] * (masked + tendency + collision))
    partial_sum = jnp.sum(sectioned[0], axis=(2, 3)).reshape(cells) / (NE * NDIR)
    density = lax.psum_scatter(partial_sum, "mom", scatter_dimension=0, tiled=True)
    return (sectioned, density)


def solution(mesh):
    placed = (P(None, "space", None, "mom", None), P("space", None), P(), P())
    return jax.shard_map(
        on_device,
        mesh=mesh,
        in_specs=placed,
        out_specs=(P(None, "space", None, "mom", None), P(("space", "mom"))),
        check_vma=False,
    )
```

```python
import functools
import math

import jax
import jax.numpy as jnp
from jax import lax
from jax.experimental import pallas as pl
from jax.experimental.pallas import tpu as pltpu
from jax.sharding import PartitionSpec as P

NE = 96
NPOL = 16
NAZ = 8
NDIR = 128
NPHON = 4
COURANT = 0.25
FLOOR = 0.1
MAX_SHIFT = 8

MESH = pl.DeviceIdType.MESH


def cosines():
    lane = lax.broadcasted_iota(jnp.int32, (8, NDIR), 1)
    polar = (lane >> 3).astype(jnp.float32)
    azimuth = lane & 7
    along = -1.0 + (2.0 * polar + 1.0) / NPOL
    big, small = math.cos(math.pi / 8), math.sin(math.pi / 8)
    outer = (azimuth == 0) | (azimuth == 3) | (azimuth == 4) | (azimuth == 7)
    size = jnp.where(outer, big, small)
    left = (azimuth >= 2) & (azimuth <= 5)
    cos_phi = jnp.where(left, -size, size)
    return along, jnp.sqrt(1.0 - along * along) * cos_phi


def lane_sums(rows):
    ones = jnp.ones((8, rows.shape[1]), jnp.bfloat16)
    high = rows.astype(jnp.bfloat16)
    low = (rows - high.astype(jnp.float32)).astype(jnp.bfloat16)
    dims = (((1,), (1,)), ((), ()))
    return lax.dot_general(ones, high, dims, preferred_element_type=jnp.float32) + lax.dot_general(
        ones, low, dims, preferred_element_type=jnp.float32
    )


def kernel(
    n_space,
    n_mom,
    dist_hbm,
    cut_ref,
    shift_ref,
    rates_ref,
    out_ref,
    dens_ref,
    dist_ref,
    masked,
    cutb,
    moments,
    gains,
    totals,
    dens_send,
    dens_recv,
    load_sem,
    halo_send,
    halo_recv,
    mom_send,
    mom_recv,
    den_send,
    den_recv,
):
    comps, nx, ne, ny, nd = dist_ref.shape
    cells = nx * ny
    reach = -(-MAX_SHIFT // ne)
    space = lax.axis_index("space")
    mom = lax.axis_index("mom")
    has_left = space > 0
    has_right = space < n_space - 1

    loads = [
        pltpu.make_async_copy(dist_hbm.at[c], dist_ref.at[c], load_sem.at[c]) for c in range(comps)
    ]
    for load in loads:
        load.start()

    barrier = pltpu.get_barrier_semaphore()

    @pl.loop(1, n_mom)
    def _(i):
        pl.semaphore_signal(
            barrier, inc=1, device_id={"mom": (mom + i) % n_mom}, device_id_type=MESH
        )

    @pl.when(has_left)
    def _():
        pl.semaphore_signal(barrier, inc=1, device_id={"space": space - 1}, device_id_type=MESH)

    @pl.when(has_right)
    def _():
        pl.semaphore_signal(barrier, inc=1, device_id={"space": space + 1}, device_id_type=MESH)

    first = mom * ne
    cut = cut_ref[...].astype(jnp.float32)
    column = lax.broadcasted_iota(jnp.int32, cut.shape, 1)

    for load in loads:
        load.wait()

    @pl.loop(0, nx)
    def _(x):
        bound = jnp.sum(jnp.where(column == x, cut, 0.0), axis=1, keepdims=True)
        bound = jnp.broadcast_to(bound, (ny, nd))
        cutb[x] = bound
        for e in range(ne):
            mask = jnp.where(bound > (first + e).astype(jnp.float32), 1.0, 0.0)
            for c in range(comps):
                masked[c, x + 1, e] = dist_ref[c, x, e] * mask

    row = lax.broadcasted_iota(jnp.int32, (8, comps * cells), 0)
    packed = jnp.zeros((8, comps * cells), jnp.float32)
    for e in range(ne):
        rows = masked[:, 1 : nx + 1, e].reshape(comps * cells, nd)
        packed = jnp.where(row == e, lane_sums(rows) * (1.0 / NDIR), packed)
    moments[reach] = packed

    @pl.when(jnp.logical_not(has_left))
    def _():
        masked[:, 0] = jnp.zeros((comps, ne, ny, nd), jnp.float32)

    @pl.when(jnp.logical_not(has_right))
    def _():
        masked[:, nx + 1] = jnp.zeros((comps, ne, ny, nd), jnp.float32)

    peers = n_mom - 1 + has_left.astype(jnp.int32) + has_right.astype(jnp.int32)
    pl.semaphore_wait(barrier, peers)

    to_left = pltpu.make_async_remote_copy(
        src_ref=masked.at[:, 1],
        dst_ref=masked.at[:, nx + 1],
        send_sem=halo_send.at[0],
        recv_sem=halo_recv.at[0],
        device_id={"space": space - 1},
        device_id_type=MESH,
    )
    to_right = pltpu.make_async_remote_copy(
        src_ref=masked.at[:, nx],
        dst_ref=masked.at[:, 0],
        send_sem=halo_send.at[1],
        recv_sem=halo_recv.at[1],
        device_id={"space": space + 1},
        device_id_type=MESH,
    )

    @pl.when(has_left)
    def _():
        to_left.start()

    @pl.when(has_right)
    def _():
        to_right.start()

    def moment_copy(offset):
        slot = reach - offset
        return pltpu.make_async_remote_copy(
            src_ref=moments.at[reach],
            dst_ref=moments.at[slot],
            send_sem=mom_send.at[slot],
            recv_sem=mom_recv.at[slot],
            device_id={"mom": mom + offset},
            device_id_type=MESH,
        )

    offsets = [o for o in range(-reach, reach + 1) if o != 0]
    for offset in offsets:
        there = (mom + offset >= 0) & (mom + offset < n_mom)

        @pl.when(there)
        def _(offset=offset):
            moment_copy(offset).start()

        @pl.when(jnp.logical_not(there))
        def _(offset=offset):
            moments[reach + offset] = jnp.zeros((8, comps * cells), jnp.float32)

    along, across = cosines()
    depth = (2 * reach + 1) * 8
    k = lax.broadcasted_iota(jnp.int32, (depth, nd), 0)
    source = (mom - reach + (k >> 3)) * ne + (k & 7)
    source = jnp.where((k & 7) < ne, source, -1000)
    weights = []
    keep = []
    speeds = []
    for e in range(ne):
        level = first + e
        weight = jnp.zeros((depth, nd), jnp.float32)
        out_rate = jnp.zeros((ny, nd), jnp.float32)
        for mode in range(NPHON):
            shift = shift_ref[mode]
            weight = weight + jnp.where(source == level - shift, rates_ref[0, mode], 0.0)
            weight = weight + jnp.where(source == level + shift, rates_ref[1, mode], 0.0)
            upper = jnp.full((ny, nd), level + shift, jnp.int32) < NE
            lower = jnp.full((ny, nd), level - shift, jnp.int32) >= 0
            out_rate = out_rate + jnp.where(upper, rates_ref[0, mode], 0.0)
            out_rate = out_rate + jnp.where(lower, rates_ref[1, mode], 0.0)
        weights.append(weight)
        keep.append(1.0 - out_rate)
        energy = jnp.full((ny, nd), level, jnp.int32).astype(jnp.float32)
        speeds.append(COURANT * jnp.sqrt((energy + 0.5) / NE))
    weights = jnp.concatenate(weights, axis=1)

    for offset in offsets:
        there = (mom + offset >= 0) & (mom + offset < n_mom)

        @pl.when(there)
        def _(offset=offset):
            moment_copy(-offset).wait_recv()

    gathered = moments[...].reshape(depth, comps * cells)
    gains[...] = lax.dot_general(
        gathered,
        weights,
        (((0,), (0,)), ((), ())),
        precision=lax.Precision.HIGHEST,
        preferred_element_type=jnp.float32,
    ).reshape(comps, nx, ny, ne * nd)

    @pl.when(has_right)
    def _():
        to_left.wait_recv()

    @pl.when(has_left)
    def _():
        to_right.wait_recv()

    y = lax.broadcasted_iota(jnp.int32, (ny, nd), 0)
    not_first = jnp.where(y > 0, 1.0, 0.0)
    not_last = jnp.where(y < ny - 1, 1.0, 0.0)

    @pl.loop(0, nx)
    def _(x):
        bound = cutb[x]
        total = jnp.zeros((ny, nd), jnp.float32)
        for e in range(ne):
            vx = speeds[e] * along
            vy = speeds[e] * across
            vp, vn = jnp.maximum(vx, 0.0), jnp.minimum(vx, 0.0)
            wp, wn = jnp.maximum(vy, 0.0), jnp.minimum(vy, 0.0)
            wp_below, wn_above = wp * not_first, wn * not_last
            m, gx, gy = masked[0, x + 1, e], masked[1, x + 1, e], masked[2, x + 1, e]
            left_x = masked[0, x, e] + masked[1, x, e]
            right_x = masked[0, x + 2, e] - masked[1, x + 2, e]
            f_right = vp * (m + gx) + vn * right_x
            f_left = vp * left_x + vn * (m - gx)
            h_right = vp * gy + vn * masked[2, x + 2, e]
            h_left = vp * masked[2, x, e] + vn * gy
            up, down = m + gy, m - gy
            p_above = wp * up + wn_above * pltpu.roll(down, ny - 1, 0)
            p_below = wp_below * pltpu.roll(up, 1, 0) + wn * down
            q_above = wp * gx + wn_above * pltpu.roll(gx, ny - 1, 0)
            q_below = wp_below * pltpu.roll(gx, 1, 0) + wn * gx
            mask = jnp.where(bound > (first + e).astype(jnp.float32), 1.0, 0.0)
            lanes = pl.ds(e * nd, nd)
            raw0 = keep[e] * m + gains[0, x, :, lanes] - (f_right - f_left) - (p_above - p_below)
            raw1 = (
                keep[e] * gx
                + gains[1, x, :, lanes]
                - 3.0 * (f_right + f_left - 2.0 * vx * m)
                - (q_above - q_below)
            )
            raw2 = (
                keep[e] * gy
                + gains[2, x, :, lanes]
                - (h_right - h_left)
                - 3.0 * (p_above + p_below - 2.0 * vy * m)
            )
            raw0, raw1, raw2 = mask * raw0, mask * raw1, mask * raw2
            spread = jnp.abs(raw1) + jnp.abs(raw2)
            scaling = jnp.minimum(1.0, jnp.maximum(raw0, 0.0) / jnp.maximum(spread, FLOOR))
            out_ref[0, x, e] = raw0
            out_ref[1, x, e] = scaling * raw1
            out_ref[2, x, e] = scaling * raw2
            total = total + raw0
        totals[x] = total

    flat = lane_sums(totals[...].reshape(cells, nd))[0:1] * (1.0 / (NE * NDIR))
    cell = lax.broadcasted_iota(jnp.int32, (nx, cells), 1)
    column_of = lax.broadcasted_iota(jnp.int32, (nx, cells), 0)
    spread_rows = jnp.where((cell // ny) == column_of, flat, 0.0)
    source_y = lax.broadcasted_iota(jnp.int32, (cells, nd), 0) % ny
    target_y = lax.broadcasted_iota(jnp.int32, (cells, nd), 1)
    pick = jnp.where(source_y == target_y, 1.0, 0.0)
    table = jnp.dot(
        spread_rows, pick, precision=lax.Precision.HIGHEST, preferred_element_type=jnp.float32
    )
    for x in range(nx):
        dens_send[x] = table[x : x + 1]

    def density_copy(target, slot):
        return pltpu.make_async_remote_copy(
            src_ref=dens_send.at[target],
            dst_ref=dens_recv.at[slot],
            send_sem=den_send.at[target],
            recv_sem=den_recv.at[slot],
            device_id={"mom": target},
            device_id_type=MESH,
        )

    @pl.loop(1, n_mom)
    def _(i):
        density_copy((mom + i) % n_mom, mom).start()

    @pl.loop(1, n_mom)
    def _(i):
        other = (mom + i) % n_mom
        density_copy(other, other).wait()

    dens_recv[mom] = dens_send[mom]
    dens_ref[...] = jnp.sum(dens_recv[...], axis=0)[:, :ny]

    for offset in offsets:
        there = (mom + offset >= 0) & (mom + offset < n_mom)

        @pl.when(there)
        def _(offset=offset):
            moment_copy(offset).wait_send()

    @pl.when(has_left)
    def _():
        to_left.wait_send()

    @pl.when(has_right)
    def _():
        to_right.wait_send()


def on_device(n_space, n_mom, distribution, cutoff, phonon_shift, phonon_rates):
    comps, nx, ny, ne, nd = distribution.shape
    reach = -(-MAX_SHIFT // ne)
    by_energy = jnp.transpose(distribution, (0, 1, 3, 2, 4))
    sectioned, density = pl.pallas_call(
        functools.partial(kernel, n_space, n_mom),
        out_shape=(
            jax.ShapeDtypeStruct((comps, nx, ne, ny, nd), jnp.float32),
            jax.ShapeDtypeStruct((1, ny), jnp.float32),
        ),
        in_specs=[
            pl.BlockSpec(memory_space=pl.ANY),
            pl.BlockSpec(memory_space=pltpu.VMEM),
            pl.BlockSpec(memory_space=pltpu.SMEM),
            pl.BlockSpec(memory_space=pltpu.SMEM),
        ],
        out_specs=(
            pl.BlockSpec(memory_space=pltpu.VMEM),
            pl.BlockSpec(memory_space=pltpu.VMEM),
        ),
        scratch_shapes=[
            pltpu.VMEM((comps, nx, ne, ny, nd), jnp.float32),
            pltpu.VMEM((comps, nx + 2, ne, ny, nd), jnp.float32),
            pltpu.VMEM((nx, ny, nd), jnp.float32),
            pltpu.VMEM((2 * reach + 1, 8, comps * nx * ny), jnp.float32),
            pltpu.VMEM((comps, nx, ny, ne * nd), jnp.float32),
            pltpu.VMEM((nx, ny, nd), jnp.float32),
            pltpu.VMEM((n_mom, 1, nd), jnp.float32),
            pltpu.VMEM((n_mom, 1, nd), jnp.float32),
            pltpu.SemaphoreType.DMA((comps,)),
            pltpu.SemaphoreType.DMA((2,)),
            pltpu.SemaphoreType.DMA((2,)),
            pltpu.SemaphoreType.DMA((2 * reach + 1,)),
            pltpu.SemaphoreType.DMA((2 * reach + 1,)),
            pltpu.SemaphoreType.DMA((n_mom,)),
            pltpu.SemaphoreType.DMA((n_mom,)),
        ],
        compiler_params=pltpu.CompilerParams(collective_id=0, has_side_effects=True),
        name="section",
    )(by_energy, jnp.transpose(cutoff), phonon_shift, phonon_rates)
    return jnp.transpose(sectioned, (0, 1, 3, 2, 4)), density.reshape(ny)


def solution(mesh):
    return jax.shard_map(
        functools.partial(on_device, mesh.shape["space"], mesh.shape["mom"]),
        mesh=mesh,
        in_specs=(P(None, "space", None, "mom", None), P("space", None), P(), P()),
        out_specs=(P(None, "space", None, "mom", None), P(("space", "mom"))),
        check_vma=False,
    )
```

```python
import functools
import math

import jax
import jax.numpy as jnp
from jax import lax
from jax.experimental import pallas as pl
from jax.experimental.pallas import tpu as pltpu
from jax.sharding import PartitionSpec as P

NE = 96
NPOL = 16
NAZ = 8
NDIR = 128
NPHON = 4
COURANT = 0.25
FLOOR = 0.1
MAX_SHIFT = 8

MESH = pl.DeviceIdType.MESH


def cosines():
    lane = lax.broadcasted_iota(jnp.int32, (8, NDIR), 1)
    polar = (lane >> 3).astype(jnp.float32)
    azimuth = lane & 7
    along = -1.0 + (2.0 * polar + 1.0) / NPOL
    big, small = math.cos(math.pi / 8), math.sin(math.pi / 8)
    outer = (azimuth == 0) | (azimuth == 3) | (azimuth == 4) | (azimuth == 7)
    size = jnp.where(outer, big, small)
    left = (azimuth >= 2) & (azimuth <= 5)
    cos_phi = jnp.where(left, -size, size)
    return along, jnp.sqrt(1.0 - along * along) * cos_phi


def lane_sums(rows):
    ones = jnp.ones((8, rows.shape[1]), jnp.bfloat16)
    high = rows.astype(jnp.bfloat16)
    low = (rows - high.astype(jnp.float32)).astype(jnp.bfloat16)
    dims = (((1,), (1,)), ((), ()))
    return lax.dot_general(ones, high, dims, preferred_element_type=jnp.float32) + lax.dot_general(
        ones, low, dims, preferred_element_type=jnp.float32
    )


def kernel(
    n_space,
    n_mom,
    dist_hbm,
    cut_ref,
    shift_ref,
    rates_ref,
    out_ref,
    dens_ref,
    dist_ref,
    masked,
    cutb,
    moments,
    gains,
    totals,
    dens_send,
    dens_recv,
    load_sem,
    halo_send,
    halo_recv,
    mom_send,
    mom_recv,
    den_send,
    den_recv,
):
    comps, nx, ne, ny, nd = dist_ref.shape
    cells = nx * ny
    reach = -(-MAX_SHIFT // ne)
    space = lax.axis_index("space")
    mom = lax.axis_index("mom")
    has_left = space > 0
    has_right = space < n_space - 1

    loads = [
        pltpu.make_async_copy(dist_hbm.at[c], dist_ref.at[c], load_sem.at[c]) for c in range(comps)
    ]
    for load in loads:
        load.start()

    barrier = pltpu.get_barrier_semaphore()

    @pl.loop(1, n_mom)
    def _(i):
        pl.semaphore_signal(
            barrier, inc=1, device_id={"mom": (mom + i) % n_mom}, device_id_type=MESH
        )

    @pl.when(has_left)
    def _():
        pl.semaphore_signal(barrier, inc=1, device_id={"space": space - 1}, device_id_type=MESH)

    @pl.when(has_right)
    def _():
        pl.semaphore_signal(barrier, inc=1, device_id={"space": space + 1}, device_id_type=MESH)

    first = mom * ne
    cut = cut_ref[...].astype(jnp.float32)
    for x in range(nx):
        cutb[x] = jnp.broadcast_to(cut[:, x : x + 1], (ny, nd))

    for load in loads:
        load.wait()

    @pl.loop(0, nx, unroll=4)
    def _(x):
        bound = cutb[x]
        for e in range(ne):
            mask = jnp.where(bound > (first + e).astype(jnp.float32), 1.0, 0.0)
            for c in range(comps):
                masked[c, x + 1, e] = dist_ref[c, x, e] * mask

    row = lax.broadcasted_iota(jnp.int32, (8, comps * cells), 0)
    packed = jnp.zeros((8, comps * cells), jnp.float32)
    for e in range(ne):
        rows = masked[:, 1 : nx + 1, e].reshape(comps * cells, nd)
        packed = jnp.where(row == e, lane_sums(rows) * (1.0 / NDIR), packed)
    moments[reach] = packed

    @pl.when(jnp.logical_not(has_left))
    def _():
        masked[:, 0] = jnp.zeros((comps, ne, ny, nd), jnp.float32)

    @pl.when(jnp.logical_not(has_right))
    def _():
        masked[:, nx + 1] = jnp.zeros((comps, ne, ny, nd), jnp.float32)

    peers = n_mom - 1 + has_left.astype(jnp.int32) + has_right.astype(jnp.int32)
    pl.semaphore_wait(barrier, peers)

    to_left = pltpu.make_async_remote_copy(
        src_ref=masked.at[:, 1],
        dst_ref=masked.at[:, nx + 1],
        send_sem=halo_send.at[0],
        recv_sem=halo_recv.at[0],
        device_id={"space": space - 1},
        device_id_type=MESH,
    )
    to_right = pltpu.make_async_remote_copy(
        src_ref=masked.at[:, nx],
        dst_ref=masked.at[:, 0],
        send_sem=halo_send.at[1],
        recv_sem=halo_recv.at[1],
        device_id={"space": space + 1},
        device_id_type=MESH,
    )

    @pl.when(has_left)
    def _():
        to_left.start()

    @pl.when(has_right)
    def _():
        to_right.start()

    def moment_copy(offset):
        slot = reach - offset
        return pltpu.make_async_remote_copy(
            src_ref=moments.at[reach],
            dst_ref=moments.at[slot],
            send_sem=mom_send.at[slot],
            recv_sem=mom_recv.at[slot],
            device_id={"mom": mom + offset},
            device_id_type=MESH,
        )

    offsets = [o for o in range(-reach, reach + 1) if o != 0]
    for offset in offsets:
        there = (mom + offset >= 0) & (mom + offset < n_mom)

        @pl.when(there)
        def _(offset=offset):
            moment_copy(offset).start()

        @pl.when(jnp.logical_not(there))
        def _(offset=offset):
            moments[reach + offset] = jnp.zeros((8, comps * cells), jnp.float32)

    along, across = cosines()
    depth = (2 * reach + 1) * 8
    k = lax.broadcasted_iota(jnp.int32, (depth, nd), 0)
    source = (mom - reach + (k >> 3)) * ne + (k & 7)
    source = jnp.where((k & 7) < ne, source, -1000)
    weights = []
    keep = []
    speeds = []
    for e in range(ne):
        level = first + e
        weight = jnp.zeros((depth, nd), jnp.float32)
        out_rate = jnp.zeros((ny, nd), jnp.float32)
        for mode in range(NPHON):
            shift = shift_ref[mode]
            weight = weight + jnp.where(source == level - shift, rates_ref[0, mode], 0.0)
            weight = weight + jnp.where(source == level + shift, rates_ref[1, mode], 0.0)
            upper = jnp.full((ny, nd), level + shift, jnp.int32) < NE
            lower = jnp.full((ny, nd), level - shift, jnp.int32) >= 0
            out_rate = out_rate + jnp.where(upper, rates_ref[0, mode], 0.0)
            out_rate = out_rate + jnp.where(lower, rates_ref[1, mode], 0.0)
        weights.append(weight)
        keep.append(1.0 - out_rate)
        energy = jnp.full((ny, nd), level, jnp.int32).astype(jnp.float32)
        speeds.append(COURANT * jnp.sqrt((energy + 0.5) / NE))
    weights = jnp.concatenate(weights, axis=1)

    y = lax.broadcasted_iota(jnp.int32, (ny, nd), 0)
    from_left = along > 0.0
    from_below = across > 0.0
    inside = jnp.where(from_below, jnp.where(y > 0, 1.0, 0.0), jnp.where(y < ny - 1, 1.0, 0.0))

    def upwind(values):
        return jnp.where(from_below, pltpu.roll(values, 1, 0), pltpu.roll(values, ny - 1, 0))

    def sources(x, e):
        before = masked[0, x, e] + masked[1, x, e]
        after = masked[0, x + 2, e] - masked[1, x + 2, e]
        m, gy = masked[0, x + 1, e], masked[2, x + 1, e]
        side_x = jnp.where(from_left, before, after)
        side_y = jnp.where(
            from_below, pltpu.roll(m + gy, 1, 0), pltpu.roll(m - gy, ny - 1, 0)
        )
        return side_x, side_y

    def mask_of(x, e):
        return jnp.where(cutb[x] > (first + e).astype(jnp.float32), 1.0, 0.0)

    def level_step(x):
        for e in range(ne):
            vx, vy = speeds[e] * along, speeds[e] * across
            ax, ay = jnp.abs(vx), jnp.abs(vy)
            side_x, side_y = sources(x, e)
            out_ref[0, x, e] = (
                (keep[e] - ax - ay) * masked[0, x + 1, e]
                - vx * masked[1, x + 1, e]
                - vy * masked[2, x + 1, e]
                + ax * side_x
                + ay * inside * side_y
            )

    pl.loop(1, nx - 1, unroll=3)(level_step)

    @pl.when(has_right)
    def _():
        to_left.wait_recv()

    @pl.when(has_left)
    def _():
        to_right.wait_recv()

    level_step(0)
    level_step(nx - 1)

    for offset in offsets:
        there = (mom + offset >= 0) & (mom + offset < n_mom)

        @pl.when(there)
        def _(offset=offset):
            moment_copy(-offset).wait_recv()

    def set_gains(c):
        gathered = moments[:, :, c * cells : (c + 1) * cells].reshape(depth, cells)
        gains[c] = lax.dot_general(
            gathered,
            weights,
            (((0,), (0,)), ((), ())),
            precision=lax.Precision.HIGHEST,
            preferred_element_type=jnp.float32,
        ).reshape(nx, ny, ne * nd)

    set_gains(0)

    @pl.loop(0, nx, unroll=4)
    def _(x):
        total = jnp.zeros((ny, nd), jnp.float32)
        for e in range(ne):
            raw0 = mask_of(x, e) * (out_ref[0, x, e] + gains[0, x, :, e * nd : (e + 1) * nd])
            out_ref[0, x, e] = raw0
            total = total + raw0
        totals[x] = total

    flat = lane_sums(totals[...].reshape(cells, nd))[0:1] * (1.0 / (NE * NDIR))
    cell = lax.broadcasted_iota(jnp.int32, (nx, cells), 1)
    column_of = lax.broadcasted_iota(jnp.int32, (nx, cells), 0)
    spread_rows = jnp.where((cell // ny) == column_of, flat, 0.0)
    source_y = lax.broadcasted_iota(jnp.int32, (cells, nd), 0) % ny
    target_y = lax.broadcasted_iota(jnp.int32, (cells, nd), 1)
    pick = jnp.where(source_y == target_y, 1.0, 0.0)
    table = jnp.dot(
        spread_rows, pick, precision=lax.Precision.HIGHEST, preferred_element_type=jnp.float32
    )
    for x in range(nx):
        dens_send[x] = table[x : x + 1]

    def density_copy(target, slot):
        return pltpu.make_async_remote_copy(
            src_ref=dens_send.at[target],
            dst_ref=dens_recv.at[slot],
            send_sem=den_send.at[target],
            recv_sem=den_recv.at[slot],
            device_id={"mom": target},
            device_id_type=MESH,
        )

    @pl.loop(1, n_mom)
    def _(i):
        density_copy((mom + i) % n_mom, mom).start()

    for c in range(1, comps):
        set_gains(c)

    @pl.loop(0, nx, unroll=2)
    def _(x):
        for e in range(ne):
            vx, vy = speeds[e] * along, speeds[e] * across
            ax, ay = jnp.abs(vx), jnp.abs(vy)
            side_x, side_y = sources(x, e)
            m, gx, gy = masked[0, x + 1, e], masked[1, x + 1, e], masked[2, x + 1, e]
            gy_side = jnp.where(from_left, masked[2, x, e], masked[2, x + 2, e])
            mask = mask_of(x, e)
            raw1 = (
                (keep[e] - 3.0 * ax - ay) * gx
                + 3.0 * vx * (m - side_x)
                + ay * inside * upwind(gx)
                + gains[1, x, :, e * nd : (e + 1) * nd]
            )
            raw2 = (
                (keep[e] - ax - 3.0 * ay) * gy
                + ax * gy_side
                + 3.0 * vy * (m - inside * side_y)
                + gains[2, x, :, e * nd : (e + 1) * nd]
            )
            raw1, raw2 = mask * raw1, mask * raw2
            spread = jnp.abs(raw1) + jnp.abs(raw2)
            raw0 = out_ref[0, x, e]
            scaling = jnp.minimum(1.0, jnp.maximum(raw0, 0.0) / jnp.maximum(spread, FLOOR))
            out_ref[1, x, e] = scaling * raw1
            out_ref[2, x, e] = scaling * raw2

    @pl.loop(1, n_mom)
    def _(i):
        other = (mom + i) % n_mom
        density_copy(other, other).wait()

    dens_recv[mom] = dens_send[mom]
    dens_ref[...] = jnp.sum(dens_recv[...], axis=0)[:, :ny]

    for offset in offsets:
        there = (mom + offset >= 0) & (mom + offset < n_mom)

        @pl.when(there)
        def _(offset=offset):
            moment_copy(offset).wait_send()

    @pl.when(has_left)
    def _():
        to_left.wait_send()

    @pl.when(has_right)
    def _():
        to_right.wait_send()


def on_device(n_space, n_mom, distribution, cutoff, phonon_shift, phonon_rates):
    comps, nx, ny, ne, nd = distribution.shape
    reach = -(-MAX_SHIFT // ne)
    by_energy = jnp.transpose(distribution, (0, 1, 3, 2, 4))
    sectioned, density = pl.pallas_call(
        functools.partial(kernel, n_space, n_mom),
        out_shape=(
            pltpu.VMEM((comps, nx, ne, ny, nd), jnp.float32),
            pltpu.VMEM((1, ny), jnp.float32),
        ),
        in_specs=[
            pl.BlockSpec(memory_space=pl.ANY),
            pl.BlockSpec(memory_space=pltpu.VMEM),
            pl.BlockSpec(memory_space=pltpu.SMEM),
            pl.BlockSpec(memory_space=pltpu.SMEM),
        ],
        out_specs=(
            pl.BlockSpec(memory_space=pltpu.VMEM),
            pl.BlockSpec(memory_space=pltpu.VMEM),
        ),
        scratch_shapes=[
            pltpu.VMEM((comps, nx, ne, ny, nd), jnp.float32),
            pltpu.VMEM((comps, nx + 2, ne, ny, nd), jnp.float32),
            pltpu.VMEM((nx, ny, nd), jnp.float32),
            pltpu.VMEM((2 * reach + 1, 8, comps * nx * ny), jnp.float32),
            pltpu.VMEM((comps, nx, ny, ne * nd), jnp.float32),
            pltpu.VMEM((nx, ny, nd), jnp.float32),
            pltpu.VMEM((n_mom, 1, nd), jnp.float32),
            pltpu.VMEM((n_mom, 1, nd), jnp.float32),
            pltpu.SemaphoreType.DMA((comps,)),
            pltpu.SemaphoreType.DMA((2,)),
            pltpu.SemaphoreType.DMA((2,)),
            pltpu.SemaphoreType.DMA((2 * reach + 1,)),
            pltpu.SemaphoreType.DMA((2 * reach + 1,)),
            pltpu.SemaphoreType.DMA((n_mom,)),
            pltpu.SemaphoreType.DMA((n_mom,)),
        ],
        compiler_params=pltpu.CompilerParams(collective_id=0, has_side_effects=True),
        name="section",
    )(by_energy, jnp.transpose(cutoff), phonon_shift, phonon_rates)
    return jnp.transpose(sectioned, (0, 1, 3, 2, 4)), density.reshape(ny)


def solution(mesh):
    return jax.shard_map(
        functools.partial(on_device, mesh.shape["space"], mesh.shape["mom"]),
        mesh=mesh,
        in_specs=(P(None, "space", None, "mom", None), P("space", None), P(), P()),
        out_specs=(P(None, "space", None, "mom", None), P(("space", "mom"))),
        check_vma=False,
    )
```

```python
import functools
import math

import jax
import jax.numpy as jnp
from jax import lax
from jax.experimental import pallas as pl
from jax.experimental.pallas import tpu as pltpu
from jax.sharding import PartitionSpec as P

NE = 96
NPOL = 16
NAZ = 8
NDIR = 128
NPHON = 4
COURANT = 0.25
FLOOR = 0.1
MAX_SHIFT = 8

MESH = pl.DeviceIdType.MESH


def cosines():
    lane = lax.broadcasted_iota(jnp.int32, (8, NDIR), 1)
    polar = (lane >> 3).astype(jnp.float32)
    azimuth = lane & 7
    along = -1.0 + (2.0 * polar + 1.0) / NPOL
    big, small = math.cos(math.pi / 8), math.sin(math.pi / 8)
    outer = (azimuth == 0) | (azimuth == 3) | (azimuth == 4) | (azimuth == 7)
    size = jnp.where(outer, big, small)
    left = (azimuth >= 2) & (azimuth <= 5)
    cos_phi = jnp.where(left, -size, size)
    return along, jnp.sqrt(1.0 - along * along) * cos_phi


def lane_sums(rows):
    ones = jnp.ones((8, rows.shape[1]), jnp.bfloat16)
    high = rows.astype(jnp.bfloat16)
    low = (rows - high.astype(jnp.float32)).astype(jnp.bfloat16)
    dims = (((1,), (1,)), ((), ()))
    return lax.dot_general(ones, high, dims, preferred_element_type=jnp.float32) + lax.dot_general(
        ones, low, dims, preferred_element_type=jnp.float32
    )


def parts(values):
    high = values.astype(jnp.bfloat16).astype(jnp.float32)
    return high, values - high


def kernel(
    n_space,
    n_mom,
    dist_hbm,
    cut_ref,
    shift_ref,
    rates_ref,
    out_ref,
    dens_ref,
    dist_ref,
    masked,
    cutb,
    moments,
    gains,
    totals,
    dens_send,
    dens_recv,
    load_sem,
    halo_send,
    halo_recv,
    mom_send,
    mom_recv,
    den_send,
    den_recv,
):
    comps, nx, ne, ny, nd = dist_ref.shape
    cells = nx * ny
    reach = -(-MAX_SHIFT // ne)
    space = lax.axis_index("space")
    mom = lax.axis_index("mom")
    has_left = space > 0
    has_right = space < n_space - 1

    loads = [
        pltpu.make_async_copy(dist_hbm.at[c], dist_ref.at[c], load_sem.at[c]) for c in range(comps)
    ]
    for load in loads:
        load.start()

    barrier = pltpu.get_barrier_semaphore()

    @pl.loop(1, n_mom)
    def _(i):
        pl.semaphore_signal(
            barrier, inc=1, device_id={"mom": (mom + i) % n_mom}, device_id_type=MESH
        )

    @pl.when(has_left)
    def _():
        pl.semaphore_signal(barrier, inc=1, device_id={"space": space - 1}, device_id_type=MESH)

    @pl.when(has_right)
    def _():
        pl.semaphore_signal(barrier, inc=1, device_id={"space": space + 1}, device_id_type=MESH)

    first = mom * ne
    cut = cut_ref[...].astype(jnp.float32)
    for x in range(nx):
        cutb[x] = jnp.broadcast_to(cut[:, x : x + 1], (ny, nd))

    for load in loads:
        load.wait()

    @pl.loop(0, nx, unroll=4)
    def _(x):
        bound = cutb[x]
        for e in range(ne):
            mask = jnp.where(bound > (first + e).astype(jnp.float32), 1.0, 0.0)
            for c in range(comps):
                masked[c, x + 1, e] = dist_ref[c, x, e] * mask

    row = lax.broadcasted_iota(jnp.int32, (8, comps * cells), 0)
    packed = jnp.zeros((8, comps * cells), jnp.float32)
    for e in range(ne):
        rows = masked[:, 1 : nx + 1, e].reshape(comps * cells, nd)
        packed = jnp.where(row == e, lane_sums(rows) * (1.0 / NDIR), packed)
    moments[reach] = packed

    along, across = cosines()
    depth = (2 * reach + 1) * 8
    k = lax.broadcasted_iota(jnp.int32, (depth, nd), 0)
    source = (mom - reach + (k >> 3)) * ne + (k & 7)
    source = jnp.where((k & 7) < ne, source, -1000)
    weights = []
    keep = []
    speeds = []
    reached = []
    for e in range(ne):
        level = first + e
        weight = jnp.zeros((depth, nd), jnp.float32)
        out_rate = jnp.zeros((ny, nd), jnp.float32)
        for mode in range(NPHON):
            shift = shift_ref[mode]
            weight = weight + jnp.where(source == level - shift, rates_ref[0, mode], 0.0)
            weight = weight + jnp.where(source == level + shift, rates_ref[1, mode], 0.0)
            upper = jnp.full((ny, nd), level + shift, jnp.int32) < NE
            lower = jnp.full((ny, nd), level - shift, jnp.int32) >= 0
            out_rate = out_rate + jnp.where(upper, rates_ref[0, mode], 0.0)
            out_rate = out_rate + jnp.where(lower, rates_ref[1, mode], 0.0)
        reached.append(
            [
                (
                    jnp.full((ny, nd), level + shift_ref[mode], jnp.int32).astype(jnp.float32),
                    jnp.full((ny, nd), level - shift_ref[mode], jnp.int32).astype(jnp.float32),
                    rates_ref[0, mode],
                    jnp.where(
                        jnp.full((ny, nd), level - shift_ref[mode], jnp.int32) >= 0,
                        rates_ref[1, mode],
                        0.0,
                    ),
                )
                for mode in range(NPHON)
            ]
        )
        weights.append(weight)
        keep.append(1.0 - out_rate)
        energy = jnp.full((ny, nd), level, jnp.int32).astype(jnp.float32)
        speeds.append(COURANT * jnp.sqrt((energy + 0.5) / NE))
    weights = jnp.concatenate(weights, axis=1)
    weights_high, weights_low = parts(weights)
    blank = jnp.zeros((8, ne * nd), jnp.float32)
    weights = jnp.concatenate([weights_high, weights_high, weights_low, blank], axis=0)
    weights = weights.astype(jnp.bfloat16)

    y = lax.broadcasted_iota(jnp.int32, (ny, nd), 0)
    from_left = along > 0.0
    from_below = across > 0.0
    inside = jnp.where(from_below, jnp.where(y > 0, 1.0, 0.0), jnp.where(y < ny - 1, 1.0, 0.0))

    def upwind(values):
        return jnp.where(from_below, pltpu.roll(values, 1, 0), pltpu.roll(values, ny - 1, 0))

    def sources(x, e):
        before = masked[0, x, e] + masked[1, x, e]
        after = masked[0, x + 2, e] - masked[1, x + 2, e]
        m, gy = masked[0, x + 1, e], masked[2, x + 1, e]
        side_x = jnp.where(from_left, before, after)
        side_y = jnp.where(
            from_below, pltpu.roll(m + gy, 1, 0), pltpu.roll(m - gy, ny - 1, 0)
        )
        return side_x, side_y

    def mask_of(x, e):
        return jnp.where(cutb[x] > (first + e).astype(jnp.float32), 1.0, 0.0)

    def level_step(x):
        bound = jnp.minimum(cutb[x], float(NE))
        total = jnp.zeros((ny, nd), jnp.float32)
        for e in range(ne):
            vx, vy = speeds[e] * along, speeds[e] * across
            ax, ay = jnp.abs(vx), jnp.abs(vy)
            side_x, side_y = sources(x, e)
            level = (
                (keep[e] - ax - ay) * masked[0, x + 1, e]
                - vx * masked[1, x + 1, e]
                - vy * masked[2, x + 1, e]
                + ax * side_x
                + ay * inside * side_y
            )
            out_ref[0, x, e] = level
            total = total + mask_of(x, e) * level
            into = jnp.zeros((ny, nd), jnp.float32)
            for mode in range(NPHON):
                above, below, absorb, emit = reached[e][mode]
                into = into + jnp.where(bound > above, absorb, 0.0)
                into = into + jnp.where(bound > below, emit, 0.0)
            total = total + into * masked[0, x + 1, e]
        totals[x] = total

    totals[0] = jnp.zeros((ny, nd), jnp.float32)
    totals[nx - 1] = jnp.zeros((ny, nd), jnp.float32)
    pl.loop(1, nx - 1, unroll=3)(level_step)

    flat = lane_sums(totals[...].reshape(cells, nd))[0:1] * (1.0 / (NE * NDIR))
    cell = lax.broadcasted_iota(jnp.int32, (nx, cells), 1)
    column_of = lax.broadcasted_iota(jnp.int32, (nx, cells), 0)
    spread_rows = jnp.where((cell // ny) == column_of, flat, 0.0)
    source_y = lax.broadcasted_iota(jnp.int32, (cells, nd), 0) % ny
    target_y = lax.broadcasted_iota(jnp.int32, (cells, nd), 1)
    pick = jnp.where(source_y == target_y, 1.0, 0.0)
    table = jnp.dot(
        spread_rows, pick, precision=lax.Precision.HIGHEST, preferred_element_type=jnp.float32
    )
    for x in range(1, nx - 1):
        dens_send[x] = table[x : x + 1]

    def density_copy(target, slot):
        return pltpu.make_async_remote_copy(
            src_ref=dens_send.at[target],
            dst_ref=dens_recv.at[slot],
            send_sem=den_send.at[target],
            recv_sem=den_recv.at[slot],
            device_id={"mom": target},
            device_id_type=MESH,
        )

    @pl.when(jnp.logical_not(has_left))
    def _():
        masked[:, 0] = jnp.zeros((comps, ne, ny, nd), jnp.float32)

    @pl.when(jnp.logical_not(has_right))
    def _():
        masked[:, nx + 1] = jnp.zeros((comps, ne, ny, nd), jnp.float32)

    peers = n_mom - 1 + has_left.astype(jnp.int32) + has_right.astype(jnp.int32)
    pl.semaphore_wait(barrier, peers)

    to_left = pltpu.make_async_remote_copy(
        src_ref=masked.at[:, 1],
        dst_ref=masked.at[:, nx + 1],
        send_sem=halo_send.at[0],
        recv_sem=halo_recv.at[0],
        device_id={"space": space - 1},
        device_id_type=MESH,
    )
    to_right = pltpu.make_async_remote_copy(
        src_ref=masked.at[:, nx],
        dst_ref=masked.at[:, 0],
        send_sem=halo_send.at[1],
        recv_sem=halo_recv.at[1],
        device_id={"space": space + 1},
        device_id_type=MESH,
    )

    @pl.when(has_left)
    def _():
        to_left.start()

    @pl.when(has_right)
    def _():
        to_right.start()

    def moment_copy(offset):
        slot = reach - offset
        return pltpu.make_async_remote_copy(
            src_ref=moments.at[reach],
            dst_ref=moments.at[slot],
            send_sem=mom_send.at[slot],
            recv_sem=mom_recv.at[slot],
            device_id={"mom": mom + offset},
            device_id_type=MESH,
        )

    offsets = [o for o in range(-reach, reach + 1) if o != 0]
    for offset in offsets:
        there = (mom + offset >= 0) & (mom + offset < n_mom)

        @pl.when(there)
        def _(offset=offset):
            moment_copy(offset).start()

        @pl.when(jnp.logical_not(there))
        def _(offset=offset):
            moments[reach + offset] = jnp.zeros((8, comps * cells), jnp.float32)

    @pl.loop(1, n_mom)
    def _(i):
        target = (mom + i) % n_mom

        @pl.when((target > 0) & (target < n_mom - 1))
        def _():
            density_copy(target, mom).start()

    @pl.when(has_right)
    def _():
        to_left.wait_recv()

    @pl.when(has_left)
    def _():
        to_right.wait_recv()

    for edge in (0, nx - 1):
        level_step(edge)
        column = jnp.concatenate([totals[edge], jnp.zeros((nd - ny, nd), jnp.float32)], axis=0)
        dens_send[edge] = lane_sums(column)[0:1] * (1.0 / (NE * NDIR))

        @pl.when(mom != edge)
        def _(edge=edge):
            density_copy(edge, mom).start()

    for offset in offsets:
        there = (mom + offset >= 0) & (mom + offset < n_mom)

        @pl.when(there)
        def _(offset=offset):
            moment_copy(-offset).wait_recv()

    def set_gains(c):
        gathered = moments[:, :, c * cells : (c + 1) * cells].reshape(depth, cells)
        high, low = parts(gathered)
        stacked = jnp.concatenate([high, low, high, jnp.zeros((8, cells), jnp.float32)], axis=0)
        gains[c] = lax.dot_general(
            stacked.astype(jnp.bfloat16),
            weights,
            (((0,), (0,)), ((), ())),
            preferred_element_type=jnp.float32,
        ).reshape(nx, ny, ne * nd)

    for c in range(comps):
        set_gains(c)

    @pl.loop(0, nx, unroll=2)
    def _(x):
        for e in range(ne):
            vx, vy = speeds[e] * along, speeds[e] * across
            ax, ay = jnp.abs(vx), jnp.abs(vy)
            side_x, side_y = sources(x, e)
            m, gx, gy = masked[0, x + 1, e], masked[1, x + 1, e], masked[2, x + 1, e]
            gy_side = jnp.where(from_left, masked[2, x, e], masked[2, x + 2, e])
            mask = mask_of(x, e)
            raw1 = (
                (keep[e] - 3.0 * ax - ay) * gx
                + 3.0 * vx * (m - side_x)
                + ay * inside * upwind(gx)
                + gains[1, x, :, e * nd : (e + 1) * nd]
            )
            raw2 = (
                (keep[e] - ax - 3.0 * ay) * gy
                + ax * gy_side
                + 3.0 * vy * (m - inside * side_y)
                + gains[2, x, :, e * nd : (e + 1) * nd]
            )
            raw1, raw2 = mask * raw1, mask * raw2
            spread = jnp.abs(raw1) + jnp.abs(raw2)
            raw0 = mask * (out_ref[0, x, e] + gains[0, x, :, e * nd : (e + 1) * nd])
            scaling = jnp.minimum(1.0, jnp.maximum(raw0, 0.0) / jnp.maximum(spread, FLOOR))
            out_ref[0, x, e] = raw0
            out_ref[1, x, e] = scaling * raw1
            out_ref[2, x, e] = scaling * raw2

    @pl.loop(1, n_mom)
    def _(i):
        other = (mom + i) % n_mom
        density_copy(other, other).wait()

    dens_recv[mom] = dens_send[mom]
    dens_ref[...] = jnp.sum(dens_recv[...], axis=0)[:, :ny]

    for offset in offsets:
        there = (mom + offset >= 0) & (mom + offset < n_mom)

        @pl.when(there)
        def _(offset=offset):
            moment_copy(offset).wait_send()

    @pl.when(has_left)
    def _():
        to_left.wait_send()

    @pl.when(has_right)
    def _():
        to_right.wait_send()


def on_device(n_space, n_mom, distribution, cutoff, phonon_shift, phonon_rates):
    comps, nx, ny, ne, nd = distribution.shape
    reach = -(-MAX_SHIFT // ne)
    by_energy = jnp.transpose(distribution, (0, 1, 3, 2, 4))
    sectioned, density = pl.pallas_call(
        functools.partial(kernel, n_space, n_mom),
        out_shape=(
            pltpu.VMEM((comps, nx, ne, ny, nd), jnp.float32),
            pltpu.VMEM((1, ny), jnp.float32),
        ),
        in_specs=[
            pl.BlockSpec(memory_space=pl.ANY),
            pl.BlockSpec(memory_space=pltpu.VMEM),
            pl.BlockSpec(memory_space=pltpu.SMEM),
            pl.BlockSpec(memory_space=pltpu.SMEM),
        ],
        out_specs=(
            pl.BlockSpec(memory_space=pltpu.VMEM),
            pl.BlockSpec(memory_space=pltpu.VMEM),
        ),
        scratch_shapes=[
            pltpu.VMEM((comps, nx, ne, ny, nd), jnp.float32),
            pltpu.VMEM((comps, nx + 2, ne, ny, nd), jnp.float32),
            pltpu.VMEM((nx, ny, nd), jnp.float32),
            pltpu.VMEM((2 * reach + 1, 8, comps * nx * ny), jnp.float32),
            pltpu.VMEM((comps, nx, ny, ne * nd), jnp.float32),
            pltpu.VMEM((nx, ny, nd), jnp.float32),
            pltpu.VMEM((n_mom, 1, nd), jnp.float32),
            pltpu.VMEM((n_mom, 1, nd), jnp.float32),
            pltpu.SemaphoreType.DMA((comps,)),
            pltpu.SemaphoreType.DMA((2,)),
            pltpu.SemaphoreType.DMA((2,)),
            pltpu.SemaphoreType.DMA((2 * reach + 1,)),
            pltpu.SemaphoreType.DMA((2 * reach + 1,)),
            pltpu.SemaphoreType.DMA((n_mom,)),
            pltpu.SemaphoreType.DMA((n_mom,)),
        ],
        compiler_params=pltpu.CompilerParams(collective_id=0, has_side_effects=True),
        name="section",
    )(by_energy, jnp.transpose(cutoff), phonon_shift, phonon_rates)
    return jnp.transpose(sectioned, (0, 1, 3, 2, 4)), density.reshape(ny)


def solution(mesh):
    return jax.shard_map(
        functools.partial(on_device, mesh.shape["space"], mesh.shape["mom"]),
        mesh=mesh,
        in_specs=(P(None, "space", None, "mom", None), P("space", None), P(), P()),
        out_specs=(P(None, "space", None, "mom", None), P(("space", "mom"))),
        check_vma=False,
    )
```

```python
import functools
import math

import jax
import jax.numpy as jnp
from jax import lax
from jax.experimental import pallas as pl
from jax.experimental.pallas import tpu as pltpu
from jax.sharding import PartitionSpec as P

NE = 96
NPOL = 16
NAZ = 8
NDIR = 128
NPHON = 4
COURANT = 0.25
FLOOR = 0.1
MAX_SHIFT = 8

MESH = pl.DeviceIdType.MESH


def cosines():
    lane = lax.broadcasted_iota(jnp.int32, (8, NDIR), 1)
    polar = (lane >> 3).astype(jnp.float32)
    azimuth = lane & 7
    along = -1.0 + (2.0 * polar + 1.0) / NPOL
    big, small = math.cos(math.pi / 8), math.sin(math.pi / 8)
    outer = (azimuth == 0) | (azimuth == 3) | (azimuth == 4) | (azimuth == 7)
    size = jnp.where(outer, big, small)
    left = (azimuth >= 2) & (azimuth <= 5)
    cos_phi = jnp.where(left, -size, size)
    return along, jnp.sqrt(1.0 - along * along) * cos_phi


def lane_sums(rows):
    ones = jnp.ones((8, rows.shape[1]), jnp.bfloat16)
    high = rows.astype(jnp.bfloat16)
    low = (rows - high.astype(jnp.float32)).astype(jnp.bfloat16)
    dims = (((1,), (1,)), ((), ()))
    return lax.dot_general(ones, high, dims, preferred_element_type=jnp.float32) + lax.dot_general(
        ones, low, dims, preferred_element_type=jnp.float32
    )


def parts(values):
    high = values.astype(jnp.bfloat16).astype(jnp.float32)
    return high, values - high


def kernel(
    n_space,
    n_mom,
    dist_hbm,
    cut_ref,
    shift_ref,
    rates_ref,
    out_ref,
    dens_ref,
    dist_ref,
    masked,
    cutb,
    moments,
    gains,
    totals,
    dens_send,
    dens_recv,
    halo_out,
    halo_in,
    load_sem,
    halo_send,
    halo_recv,
    mom_send,
    mom_recv,
    den_send,
    den_recv,
):
    comps, nx, ne, ny, nd = dist_ref.shape
    cells = nx * ny
    reach = -(-MAX_SHIFT // ne)
    space = lax.axis_index("space")
    mom = lax.axis_index("mom")
    has_left = space > 0
    has_right = space < n_space - 1

    loads = [
        pltpu.make_async_copy(dist_hbm.at[c], dist_ref.at[c], load_sem.at[c]) for c in range(comps)
    ]
    for load in loads:
        load.start()

    barrier = pltpu.get_barrier_semaphore()

    @pl.loop(1, n_mom)
    def _(i):
        pl.semaphore_signal(
            barrier, inc=1, device_id={"mom": (mom + i) % n_mom}, device_id_type=MESH
        )

    @pl.when(has_left)
    def _():
        pl.semaphore_signal(barrier, inc=1, device_id={"space": space - 1}, device_id_type=MESH)

    @pl.when(has_right)
    def _():
        pl.semaphore_signal(barrier, inc=1, device_id={"space": space + 1}, device_id_type=MESH)

    first = mom * ne
    cut = cut_ref[...].astype(jnp.float32)
    for x in range(nx):
        cutb[x] = jnp.broadcast_to(cut[:, x : x + 1], (ny, nd))

    for load in loads:
        load.wait()

    @pl.loop(0, nx, unroll=4)
    def _(x):
        bound = cutb[x]
        for e in range(ne):
            mask = jnp.where(bound > (first + e).astype(jnp.float32), 1.0, 0.0)
            for c in range(comps):
                masked[c, x + 1, e] = dist_ref[c, x, e] * mask

    row = lax.broadcasted_iota(jnp.int32, (8, comps * cells), 0)
    packed = jnp.zeros((8, comps * cells), jnp.float32)
    for e in range(ne):
        rows = masked[:, 1 : nx + 1, e].reshape(comps * cells, nd)
        packed = jnp.where(row == e, lane_sums(rows) * (1.0 / NDIR), packed)
    moments[reach] = packed[0:4]
    upper = lax.broadcasted_iota(jnp.int32, (ny, nd), 1) >= nd // 2
    for e in range(ne):
        m, gx, gy = (masked[c, 1, e] for c in range(comps))
        halo_out[0, e] = jnp.where(upper, pltpu.roll(gy, nd // 2, 1), m - gx)
        m, gx, gy = (masked[c, nx, e] for c in range(comps))
        halo_out[1, e] = jnp.where(upper, m + gx, pltpu.roll(gy, nd // 2, 1))

    along, across = cosines()
    depth = (2 * reach + 1) * 8
    k = lax.broadcasted_iota(jnp.int32, (depth, nd), 0)
    source = (mom - reach + (k >> 3)) * ne + (k & 7)
    source = jnp.where((k & 7) < ne, source, -1000)
    weights = []
    keep = []
    speeds = []
    reached = []
    for e in range(ne):
        level = first + e
        weight = jnp.zeros((depth, nd), jnp.float32)
        out_rate = jnp.zeros((ny, nd), jnp.float32)
        for mode in range(NPHON):
            shift = shift_ref[mode]
            weight = weight + jnp.where(source == level - shift, rates_ref[0, mode], 0.0)
            weight = weight + jnp.where(source == level + shift, rates_ref[1, mode], 0.0)
            upper = jnp.full((ny, nd), level + shift, jnp.int32) < NE
            lower = jnp.full((ny, nd), level - shift, jnp.int32) >= 0
            out_rate = out_rate + jnp.where(upper, rates_ref[0, mode], 0.0)
            out_rate = out_rate + jnp.where(lower, rates_ref[1, mode], 0.0)
        reached.append(
            [
                (
                    jnp.full((ny, nd), level + shift_ref[mode], jnp.int32).astype(jnp.float32),
                    jnp.full((ny, nd), level - shift_ref[mode], jnp.int32).astype(jnp.float32),
                    rates_ref[0, mode],
                    jnp.where(
                        jnp.full((ny, nd), level - shift_ref[mode], jnp.int32) >= 0,
                        rates_ref[1, mode],
                        0.0,
                    ),
                )
                for mode in range(NPHON)
            ]
        )
        weights.append(weight)
        keep.append(1.0 - out_rate)
        energy = jnp.full((ny, nd), level, jnp.int32).astype(jnp.float32)
        speeds.append(COURANT * jnp.sqrt((energy + 0.5) / NE))
    weights = jnp.concatenate(weights, axis=1)
    weights_high, weights_low = parts(weights)
    blank = jnp.zeros((8, ne * nd), jnp.float32)
    weights = jnp.concatenate([weights_high, weights_high, weights_low, blank], axis=0)
    weights = weights.astype(jnp.bfloat16)

    y = lax.broadcasted_iota(jnp.int32, (ny, nd), 0)
    from_left = along > 0.0
    from_below = across > 0.0
    inside = jnp.where(from_below, jnp.where(y > 0, 1.0, 0.0), jnp.where(y < ny - 1, 1.0, 0.0))

    def upwind(values):
        return jnp.where(from_below, pltpu.roll(values, 1, 0), pltpu.roll(values, ny - 1, 0))

    def sources(x, e):
        before = masked[0, x, e] + masked[1, x, e]
        after = masked[0, x + 2, e] - masked[1, x + 2, e]
        m, gy = masked[0, x + 1, e], masked[2, x + 1, e]
        side_x = jnp.where(from_left, before, after)
        side_y = jnp.where(
            from_below, pltpu.roll(m + gy, 1, 0), pltpu.roll(m - gy, ny - 1, 0)
        )
        return side_x, side_y

    def mask_of(x, e):
        return jnp.where(cutb[x] > (first + e).astype(jnp.float32), 1.0, 0.0)

    def level_step(x):
        bound = jnp.minimum(cutb[x], float(NE))
        total = jnp.zeros((ny, nd), jnp.float32)
        for e in range(ne):
            vx, vy = speeds[e] * along, speeds[e] * across
            ax, ay = jnp.abs(vx), jnp.abs(vy)
            side_x, side_y = sources(x, e)
            level = (
                (keep[e] - ax - ay) * masked[0, x + 1, e]
                - vx * masked[1, x + 1, e]
                - vy * masked[2, x + 1, e]
                + ax * side_x
                + ay * inside * side_y
            )
            out_ref[0, x, e] = level
            total = total + mask_of(x, e) * level
            into = jnp.zeros((ny, nd), jnp.float32)
            for mode in range(NPHON):
                above, below, absorb, emit = reached[e][mode]
                into = into + jnp.where(bound > above, absorb, 0.0)
                into = into + jnp.where(bound > below, emit, 0.0)
            total = total + into * masked[0, x + 1, e]
        totals[x] = total

    totals[0] = jnp.zeros((ny, nd), jnp.float32)
    totals[nx - 1] = jnp.zeros((ny, nd), jnp.float32)
    pl.loop(1, nx - 1, unroll=3)(level_step)

    flat = lane_sums(totals[...].reshape(cells, nd))[0:1] * (1.0 / (NE * NDIR))
    cell = lax.broadcasted_iota(jnp.int32, (nx, cells), 1)
    column_of = lax.broadcasted_iota(jnp.int32, (nx, cells), 0)
    spread_rows = jnp.where((cell // ny) == column_of, flat, 0.0)
    source_y = lax.broadcasted_iota(jnp.int32, (cells, nd), 0) % ny
    target_y = lax.broadcasted_iota(jnp.int32, (cells, nd), 1)
    pick = jnp.where(source_y == target_y, 1.0, 0.0)
    table = jnp.dot(
        spread_rows, pick, precision=lax.Precision.HIGHEST, preferred_element_type=jnp.float32
    )
    for x in range(1, nx - 1):
        dens_send[x] = table[x : x + 1]

    def density_copy(target, slot):
        return pltpu.make_async_remote_copy(
            src_ref=dens_send.at[target],
            dst_ref=dens_recv.at[slot],
            send_sem=den_send.at[target],
            recv_sem=den_recv.at[slot],
            device_id={"mom": target},
            device_id_type=MESH,
        )

    @pl.when(jnp.logical_not(has_left))
    def _():
        halo_in[1] = jnp.zeros((ne, ny, nd), jnp.float32)

    @pl.when(jnp.logical_not(has_right))
    def _():
        halo_in[0] = jnp.zeros((ne, ny, nd), jnp.float32)

    peers = n_mom - 1 + has_left.astype(jnp.int32) + has_right.astype(jnp.int32)
    pl.semaphore_wait(barrier, peers)

    to_left = pltpu.make_async_remote_copy(
        src_ref=halo_out.at[0],
        dst_ref=halo_in.at[0],
        send_sem=halo_send.at[0],
        recv_sem=halo_recv.at[0],
        device_id={"space": space - 1},
        device_id_type=MESH,
    )
    to_right = pltpu.make_async_remote_copy(
        src_ref=halo_out.at[1],
        dst_ref=halo_in.at[1],
        send_sem=halo_send.at[1],
        recv_sem=halo_recv.at[1],
        device_id={"space": space + 1},
        device_id_type=MESH,
    )

    @pl.when(has_left)
    def _():
        to_left.start()

    @pl.when(has_right)
    def _():
        to_right.start()

    def moment_copy(offset):
        slot = reach - offset
        return pltpu.make_async_remote_copy(
            src_ref=moments.at[reach],
            dst_ref=moments.at[slot],
            send_sem=mom_send.at[slot],
            recv_sem=mom_recv.at[slot],
            device_id={"mom": mom + offset},
            device_id_type=MESH,
        )

    @pl.loop(1, n_mom)
    def _(i):
        target = (mom + i) % n_mom

        @pl.when((target > 0) & (target < n_mom - 1))
        def _():
            density_copy(target, mom).start()

    offsets = [o for o in range(-reach, reach + 1) if o != 0]
    for offset in offsets:
        there = (mom + offset >= 0) & (mom + offset < n_mom)

        @pl.when(there)
        def _(offset=offset):
            moment_copy(offset).start()

        @pl.when(jnp.logical_not(there))
        def _(offset=offset):
            moments[reach + offset] = jnp.zeros((4, comps * cells), jnp.float32)

    @pl.when(has_right)
    def _():
        to_left.wait_recv()

    @pl.when(has_left)
    def _():
        to_right.wait_recv()

    for side, place in ((1, 0), (0, nx + 1)):
        for e in range(ne):
            arrived = halo_in[side, e]
            masked[0, place, e] = arrived
            masked[1, place, e] = jnp.zeros((ny, nd), jnp.float32)
            masked[2, place, e] = pltpu.roll(arrived, nd // 2, 1)

    for edge in (0, nx - 1):
        level_step(edge)
        column = jnp.concatenate([totals[edge], jnp.zeros((nd - ny, nd), jnp.float32)], axis=0)
        dens_send[edge] = lane_sums(column)[0:1] * (1.0 / (NE * NDIR))

        @pl.when(mom != edge)
        def _(edge=edge):
            density_copy(edge, mom).start()

    for offset in offsets:
        there = (mom + offset >= 0) & (mom + offset < n_mom)

        @pl.when(there)
        def _(offset=offset):
            moment_copy(-offset).wait_recv()

    def set_gains(c):
        gathered = moments[:, :, c * cells : (c + 1) * cells]
        gathered = jnp.concatenate([gathered, jnp.zeros_like(gathered)], axis=1).reshape(depth, cells)
        high, low = parts(gathered)
        stacked = jnp.concatenate([high, low, high, jnp.zeros((8, cells), jnp.float32)], axis=0)
        gains[c] = lax.dot_general(
            stacked.astype(jnp.bfloat16),
            weights,
            (((0,), (0,)), ((), ())),
            preferred_element_type=jnp.float32,
        ).reshape(nx, ny, ne * nd)

    for c in range(comps):
        set_gains(c)

    @pl.loop(0, nx, unroll=2)
    def _(x):
        for e in range(ne):
            vx, vy = speeds[e] * along, speeds[e] * across
            ax, ay = jnp.abs(vx), jnp.abs(vy)
            side_x, side_y = sources(x, e)
            m, gx, gy = masked[0, x + 1, e], masked[1, x + 1, e], masked[2, x + 1, e]
            gy_side = jnp.where(from_left, masked[2, x, e], masked[2, x + 2, e])
            mask = mask_of(x, e)
            raw1 = (
                (keep[e] - 3.0 * ax - ay) * gx
                + 3.0 * vx * (m - side_x)
                + ay * inside * upwind(gx)
                + gains[1, x, :, e * nd : (e + 1) * nd]
            )
            raw2 = (
                (keep[e] - ax - 3.0 * ay) * gy
                + ax * gy_side
                + 3.0 * vy * (m - inside * side_y)
                + gains[2, x, :, e * nd : (e + 1) * nd]
            )
            raw1, raw2 = mask * raw1, mask * raw2
            spread = jnp.abs(raw1) + jnp.abs(raw2)
            raw0 = mask * (out_ref[0, x, e] + gains[0, x, :, e * nd : (e + 1) * nd])
            scaling = jnp.minimum(1.0, jnp.maximum(raw0, 0.0) / jnp.maximum(spread, FLOOR))
            out_ref[0, x, e] = raw0
            out_ref[1, x, e] = scaling * raw1
            out_ref[2, x, e] = scaling * raw2

    @pl.loop(1, n_mom)
    def _(i):
        other = (mom + i) % n_mom
        density_copy(other, other).wait()

    dens_recv[mom] = dens_send[mom]
    dens_ref[...] = jnp.sum(dens_recv[...], axis=0)[:, :ny]

    for offset in offsets:
        there = (mom + offset >= 0) & (mom + offset < n_mom)

        @pl.when(there)
        def _(offset=offset):
            moment_copy(offset).wait_send()

    @pl.when(has_left)
    def _():
        to_left.wait_send()

    @pl.when(has_right)
    def _():
        to_right.wait_send()


def on_device(n_space, n_mom, distribution, cutoff, phonon_shift, phonon_rates):
    comps, nx, ny, ne, nd = distribution.shape
    reach = -(-MAX_SHIFT // ne)
    by_energy = jnp.transpose(distribution, (0, 1, 3, 2, 4))
    sectioned, density = pl.pallas_call(
        functools.partial(kernel, n_space, n_mom),
        out_shape=(
            pltpu.VMEM((comps, nx, ne, ny, nd), jnp.float32),
            pltpu.VMEM((1, ny), jnp.float32),
        ),
        in_specs=[
            pl.BlockSpec(memory_space=pl.ANY),
            pl.BlockSpec(memory_space=pltpu.VMEM),
            pl.BlockSpec(memory_space=pltpu.SMEM),
            pl.BlockSpec(memory_space=pltpu.SMEM),
        ],
        out_specs=(
            pl.BlockSpec(memory_space=pltpu.VMEM),
            pl.BlockSpec(memory_space=pltpu.VMEM),
        ),
        scratch_shapes=[
            pltpu.VMEM((comps, nx, ne, ny, nd), jnp.float32),
            pltpu.VMEM((comps, nx + 2, ne, ny, nd), jnp.float32),
            pltpu.VMEM((nx, ny, nd), jnp.float32),
            pltpu.VMEM((2 * reach + 1, 4, comps * nx * ny), jnp.float32),
            pltpu.VMEM((comps, nx, ny, ne * nd), jnp.float32),
            pltpu.VMEM((nx, ny, nd), jnp.float32),
            pltpu.VMEM((n_mom, 1, nd), jnp.float32),
            pltpu.VMEM((n_mom, 1, nd), jnp.float32),
            pltpu.VMEM((2, ne, ny, nd), jnp.float32),
            pltpu.VMEM((2, ne, ny, nd), jnp.float32),
            pltpu.SemaphoreType.DMA((comps,)),
            pltpu.SemaphoreType.DMA((2,)),
            pltpu.SemaphoreType.DMA((2,)),
            pltpu.SemaphoreType.DMA((2 * reach + 1,)),
            pltpu.SemaphoreType.DMA((2 * reach + 1,)),
            pltpu.SemaphoreType.DMA((n_mom,)),
            pltpu.SemaphoreType.DMA((n_mom,)),
        ],
        compiler_params=pltpu.CompilerParams(collective_id=0, has_side_effects=True),
        name="section",
    )(by_energy, jnp.transpose(cutoff), phonon_shift, phonon_rates)
    return jnp.transpose(sectioned, (0, 1, 3, 2, 4)), density.reshape(ny)


def solution(mesh):
    return jax.shard_map(
        functools.partial(on_device, mesh.shape["space"], mesh.shape["mom"]),
        mesh=mesh,
        in_specs=(P(None, "space", None, "mom", None), P("space", None), P(), P()),
        out_specs=(P(None, "space", None, "mom", None), P(("space", "mom"))),
        check_vma=False,
    )
```

```python
import functools
import math

import jax
import jax.numpy as jnp
from jax import lax
from jax.experimental import pallas as pl
from jax.experimental.pallas import tpu as pltpu
from jax.sharding import PartitionSpec as P

NE = 96
NPOL = 16
NAZ = 8
NDIR = 128
NPHON = 4
COURANT = 0.25
FLOOR = 0.1
MAX_SHIFT = 8

MESH = pl.DeviceIdType.MESH


def cosines():
    lane = lax.broadcasted_iota(jnp.int32, (8, NDIR), 1)
    polar = (lane >> 3).astype(jnp.float32)
    azimuth = lane & 7
    along = -1.0 + (2.0 * polar + 1.0) / NPOL
    big, small = math.cos(math.pi / 8), math.sin(math.pi / 8)
    outer = (azimuth == 0) | (azimuth == 3) | (azimuth == 4) | (azimuth == 7)
    size = jnp.where(outer, big, small)
    left = (azimuth >= 2) & (azimuth <= 5)
    cos_phi = jnp.where(left, -size, size)
    return along, jnp.sqrt(1.0 - along * along) * cos_phi


def lane_sums(rows):
    ones = jnp.ones((8, rows.shape[1]), jnp.bfloat16)
    high = rows.astype(jnp.bfloat16)
    low = (rows - high.astype(jnp.float32)).astype(jnp.bfloat16)
    dims = (((1,), (1,)), ((), ()))
    return lax.dot_general(ones, high, dims, preferred_element_type=jnp.float32) + lax.dot_general(
        ones, low, dims, preferred_element_type=jnp.float32
    )


def parts(values):
    high = values.astype(jnp.bfloat16).astype(jnp.float32)
    return high, values - high


def kernel(
    n_space,
    n_mom,
    dist_hbm,
    cut_ref,
    shift_ref,
    rates_ref,
    out_ref,
    dens_ref,
    dist_ref,
    masked,
    cutb,
    moments,
    gains,
    totals,
    dens_send,
    dens_recv,
    halo_out,
    halo_in,
    load_sem,
    halo_send,
    halo_recv,
    mom_send,
    mom_recv,
    den_send,
    den_recv,
):
    comps, nx, ne, ny, nd = dist_ref.shape
    cells = nx * ny
    reach = -(-MAX_SHIFT // ne)
    space = lax.axis_index("space")
    mom = lax.axis_index("mom")
    has_left = space > 0
    has_right = space < n_space - 1

    loads = [
        pltpu.make_async_copy(dist_hbm.at[c], dist_ref.at[c], load_sem.at[c]) for c in range(comps)
    ]
    for load in loads:
        load.start()

    barrier = pltpu.get_barrier_semaphore()

    @pl.loop(1, n_mom)
    def _(i):
        pl.semaphore_signal(
            barrier, inc=1, device_id={"mom": (mom + i) % n_mom}, device_id_type=MESH
        )

    @pl.when(has_left)
    def _():
        pl.semaphore_signal(barrier, inc=1, device_id={"space": space - 1}, device_id_type=MESH)

    @pl.when(has_right)
    def _():
        pl.semaphore_signal(barrier, inc=1, device_id={"space": space + 1}, device_id_type=MESH)

    first = mom * ne
    cut = cut_ref[...].astype(jnp.float32)
    for x in range(nx):
        cutb[x] = jnp.broadcast_to(cut[:, x : x + 1], (ny, nd))

    for load in loads:
        load.wait()

    @pl.loop(0, nx, unroll=4)
    def _(x):
        bound = cutb[x]
        for e in range(ne):
            mask = jnp.where(bound > (first + e).astype(jnp.float32), 1.0, 0.0)
            for c in range(comps):
                masked[c, x + 1, e] = dist_ref[c, x, e] * mask

    row = lax.broadcasted_iota(jnp.int32, (8, comps * cells), 0)
    packed = jnp.zeros((8, comps * cells), jnp.float32)
    for e in range(ne):
        rows = masked[:, 1 : nx + 1, e].reshape(comps * cells, nd)
        packed = jnp.where(row == e, lane_sums(rows) * (1.0 / NDIR), packed)
    moments[reach] = packed[0:4]
    upper = lax.broadcasted_iota(jnp.int32, (ny, nd), 1) >= nd // 2
    for e in range(ne):
        m, gx, gy = (masked[c, 1, e] for c in range(comps))
        halo_out[0, e] = jnp.where(upper, pltpu.roll(gy, nd // 2, 1), m - gx)
        m, gx, gy = (masked[c, nx, e] for c in range(comps))
        halo_out[1, e] = jnp.where(upper, m + gx, pltpu.roll(gy, nd // 2, 1))

    along, across = cosines()
    depth = (2 * reach + 1) * 8
    k = lax.broadcasted_iota(jnp.int32, (depth, nd), 0)
    source = (mom - reach + (k >> 3)) * ne + (k & 7)
    source = jnp.where((k & 7) < ne, source, -1000)
    weights = []
    keep = []
    speeds = []
    reached = []
    for e in range(ne):
        level = first + e
        weight = jnp.zeros((depth, nd), jnp.float32)
        out_rate = jnp.zeros((ny, nd), jnp.float32)
        for mode in range(NPHON):
            shift = shift_ref[mode]
            weight = weight + jnp.where(source == level - shift, rates_ref[0, mode], 0.0)
            weight = weight + jnp.where(source == level + shift, rates_ref[1, mode], 0.0)
            upper = jnp.full((ny, nd), level + shift, jnp.int32) < NE
            lower = jnp.full((ny, nd), level - shift, jnp.int32) >= 0
            out_rate = out_rate + jnp.where(upper, rates_ref[0, mode], 0.0)
            out_rate = out_rate + jnp.where(lower, rates_ref[1, mode], 0.0)
        reached.append(
            [
                (
                    jnp.full((ny, nd), level + shift_ref[mode], jnp.int32).astype(jnp.float32),
                    jnp.full((ny, nd), level - shift_ref[mode], jnp.int32).astype(jnp.float32),
                    rates_ref[0, mode],
                    jnp.where(
                        jnp.full((ny, nd), level - shift_ref[mode], jnp.int32) >= 0,
                        rates_ref[1, mode],
                        0.0,
                    ),
                )
                for mode in range(NPHON)
            ]
        )
        weights.append(weight)
        keep.append(1.0 - out_rate)
        energy = jnp.full((ny, nd), level, jnp.int32).astype(jnp.float32)
        speeds.append(COURANT * jnp.sqrt((energy + 0.5) / NE))
    weights = jnp.concatenate(weights, axis=1)
    weights_high, weights_low = parts(weights)
    blank = jnp.zeros((8, ne * nd), jnp.float32)
    weights = jnp.concatenate([weights_high, weights_high, weights_low, blank], axis=0)
    weights = weights.astype(jnp.bfloat16)

    y = lax.broadcasted_iota(jnp.int32, (ny, nd), 0)
    from_left = along > 0.0
    from_below = across > 0.0
    inside = jnp.where(from_below, jnp.where(y > 0, 1.0, 0.0), jnp.where(y < ny - 1, 1.0, 0.0))

    def upwind(values):
        return jnp.where(from_below, pltpu.roll(values, 1, 0), pltpu.roll(values, ny - 1, 0))

    def sources(x, e):
        before = masked[0, x, e] + masked[1, x, e]
        after = masked[0, x + 2, e] - masked[1, x + 2, e]
        m, gy = masked[0, x + 1, e], masked[2, x + 1, e]
        side_x = jnp.where(from_left, before, after)
        side_y = jnp.where(
            from_below, pltpu.roll(m + gy, 1, 0), pltpu.roll(m - gy, ny - 1, 0)
        )
        return side_x, side_y

    def mask_of(x, e):
        return jnp.where(cutb[x] > (first + e).astype(jnp.float32), 1.0, 0.0)

    def level_step(x):
        bound = jnp.minimum(cutb[x], float(NE))
        total = jnp.zeros((ny, nd), jnp.float32)
        for e in range(ne):
            vx, vy = speeds[e] * along, speeds[e] * across
            ax, ay = jnp.abs(vx), jnp.abs(vy)
            side_x, side_y = sources(x, e)
            level = (
                (keep[e] - ax - ay) * masked[0, x + 1, e]
                - vx * masked[1, x + 1, e]
                - vy * masked[2, x + 1, e]
                + ax * side_x
                + ay * inside * side_y
            )
            out_ref[0, x, e] = level
            total = total + mask_of(x, e) * level
            into = jnp.zeros((ny, nd), jnp.float32)
            for mode in range(NPHON):
                above, below, absorb, emit = reached[e][mode]
                into = into + jnp.where(bound > above, absorb, 0.0)
                into = into + jnp.where(bound > below, emit, 0.0)
            total = total + into * masked[0, x + 1, e]
        totals[x] = total

    totals[0] = jnp.zeros((ny, nd), jnp.float32)
    totals[nx - 1] = jnp.zeros((ny, nd), jnp.float32)
    pl.loop(1, nx - 1, unroll=3)(level_step)

    flat = lane_sums(totals[...].reshape(cells, nd))[0:1] * (1.0 / (NE * NDIR))
    cell = lax.broadcasted_iota(jnp.int32, (nx, cells), 1)
    column_of = lax.broadcasted_iota(jnp.int32, (nx, cells), 0)
    spread_rows = jnp.where((cell // ny) == column_of, flat, 0.0)
    source_y = lax.broadcasted_iota(jnp.int32, (cells, nd), 0) % ny
    target_y = lax.broadcasted_iota(jnp.int32, (cells, nd), 1)
    pick = jnp.where(source_y == target_y, 1.0, 0.0)
    table = jnp.dot(
        spread_rows, pick, precision=lax.Precision.HIGHEST, preferred_element_type=jnp.float32
    )
    for x in range(1, nx - 1):
        dens_send[x] = table[x : x + 1]

    def density_copy(target, slot):
        return pltpu.make_async_remote_copy(
            src_ref=dens_send.at[target],
            dst_ref=dens_recv.at[slot],
            send_sem=den_send.at[target],
            recv_sem=den_recv.at[slot],
            device_id={"mom": target},
            device_id_type=MESH,
        )

    @pl.when(jnp.logical_not(has_left))
    def _():
        halo_in[1] = jnp.zeros((ne, ny, nd), jnp.float32)

    @pl.when(jnp.logical_not(has_right))
    def _():
        halo_in[0] = jnp.zeros((ne, ny, nd), jnp.float32)

    peers = n_mom - 1 + has_left.astype(jnp.int32) + has_right.astype(jnp.int32)
    pl.semaphore_wait(barrier, peers)

    to_left = pltpu.make_async_remote_copy(
        src_ref=halo_out.at[0],
        dst_ref=halo_in.at[0],
        send_sem=halo_send.at[0],
        recv_sem=halo_recv.at[0],
        device_id={"space": space - 1},
        device_id_type=MESH,
    )
    to_right = pltpu.make_async_remote_copy(
        src_ref=halo_out.at[1],
        dst_ref=halo_in.at[1],
        send_sem=halo_send.at[1],
        recv_sem=halo_recv.at[1],
        device_id={"space": space + 1},
        device_id_type=MESH,
    )

    @pl.when(has_left)
    def _():
        to_left.start()

    @pl.when(has_right)
    def _():
        to_right.start()

    def moment_copy(offset):
        slot = reach - offset
        return pltpu.make_async_remote_copy(
            src_ref=moments.at[reach],
            dst_ref=moments.at[slot],
            send_sem=mom_send.at[slot],
            recv_sem=mom_recv.at[slot],
            device_id={"mom": mom + offset},
            device_id_type=MESH,
        )

    @pl.loop(1, n_mom)
    def _(i):
        target = (mom + i) % n_mom

        @pl.when((target > 0) & (target < n_mom - 1))
        def _():
            density_copy(target, mom).start()

    offsets = [o for o in range(-reach, reach + 1) if o != 0]
    for offset in offsets:
        there = (mom + offset >= 0) & (mom + offset < n_mom)

        @pl.when(there)
        def _(offset=offset):
            moment_copy(offset).start()

        @pl.when(jnp.logical_not(there))
        def _(offset=offset):
            moments[reach + offset] = jnp.zeros((4, comps * cells), jnp.float32)

    @pl.when(has_right)
    def _():
        to_left.wait_recv()

    @pl.when(has_left)
    def _():
        to_right.wait_recv()

    for side, place in ((1, 0), (0, nx + 1)):
        for e in range(ne):
            arrived = halo_in[side, e]
            masked[0, place, e] = arrived
            masked[1, place, e] = jnp.zeros((ny, nd), jnp.float32)
            masked[2, place, e] = pltpu.roll(arrived, nd // 2, 1)

    edges = (0, nx - 1)
    blank_rows = jnp.zeros((nd - ny, nd), jnp.float32)
    for edge in edges:
        level_step(edge)
    columns = [jnp.concatenate([totals[edge], blank_rows], axis=0) for edge in edges]
    for edge, column in zip(edges, columns):
        dens_send[edge] = lane_sums(column)[0:1] * (1.0 / (NE * NDIR))

    for edge in edges:

        @pl.when(mom != edge)
        def _(edge=edge):
            density_copy(edge, mom).start()

    for offset in offsets:
        there = (mom + offset >= 0) & (mom + offset < n_mom)

        @pl.when(there)
        def _(offset=offset):
            moment_copy(-offset).wait_recv()

    def set_gains(c):
        gathered = moments[:, :, c * cells : (c + 1) * cells]
        gathered = jnp.concatenate([gathered, jnp.zeros_like(gathered)], axis=1).reshape(depth, cells)
        high, low = parts(gathered)
        stacked = jnp.concatenate([high, low, high, jnp.zeros((8, cells), jnp.float32)], axis=0)
        gains[c] = lax.dot_general(
            stacked.astype(jnp.bfloat16),
            weights,
            (((0,), (0,)), ((), ())),
            preferred_element_type=jnp.float32,
        ).reshape(nx, ny, ne * nd)

    for c in range(comps):
        set_gains(c)

    @pl.loop(0, nx, unroll=2)
    def _(x):
        for e in range(ne):
            vx, vy = speeds[e] * along, speeds[e] * across
            ax, ay = jnp.abs(vx), jnp.abs(vy)
            side_x, side_y = sources(x, e)
            m, gx, gy = masked[0, x + 1, e], masked[1, x + 1, e], masked[2, x + 1, e]
            gy_side = jnp.where(from_left, masked[2, x, e], masked[2, x + 2, e])
            mask = mask_of(x, e)
            raw1 = (
                (keep[e] - 3.0 * ax - ay) * gx
                + 3.0 * vx * (m - side_x)
                + ay * inside * upwind(gx)
                + gains[1, x, :, e * nd : (e + 1) * nd]
            )
            raw2 = (
                (keep[e] - ax - 3.0 * ay) * gy
                + ax * gy_side
                + 3.0 * vy * (m - inside * side_y)
                + gains[2, x, :, e * nd : (e + 1) * nd]
            )
            raw1, raw2 = mask * raw1, mask * raw2
            spread = jnp.abs(raw1) + jnp.abs(raw2)
            raw0 = mask * (out_ref[0, x, e] + gains[0, x, :, e * nd : (e + 1) * nd])
            scaling = jnp.minimum(1.0, jnp.maximum(raw0, 0.0) / jnp.maximum(spread, FLOOR))
            out_ref[0, x, e] = raw0
            out_ref[1, x, e] = scaling * raw1
            out_ref[2, x, e] = scaling * raw2

    @pl.loop(1, n_mom)
    def _(i):
        other = (mom + i) % n_mom
        density_copy(other, other).wait()

    dens_recv[mom] = dens_send[mom]
    dens_ref[...] = jnp.sum(dens_recv[...], axis=0)[:, :ny]

    for offset in offsets:
        there = (mom + offset >= 0) & (mom + offset < n_mom)

        @pl.when(there)
        def _(offset=offset):
            moment_copy(offset).wait_send()

    @pl.when(has_left)
    def _():
        to_left.wait_send()

    @pl.when(has_right)
    def _():
        to_right.wait_send()


def on_device(n_space, n_mom, distribution, cutoff, phonon_shift, phonon_rates):
    comps, nx, ny, ne, nd = distribution.shape
    reach = -(-MAX_SHIFT // ne)
    by_energy = jnp.transpose(distribution, (0, 1, 3, 2, 4))
    sectioned, density = pl.pallas_call(
        functools.partial(kernel, n_space, n_mom),
        out_shape=(
            pltpu.VMEM((comps, nx, ne, ny, nd), jnp.float32),
            pltpu.VMEM((1, ny), jnp.float32),
        ),
        in_specs=[
            pl.BlockSpec(memory_space=pl.ANY),
            pl.BlockSpec(memory_space=pltpu.VMEM),
            pl.BlockSpec(memory_space=pltpu.SMEM),
            pl.BlockSpec(memory_space=pltpu.SMEM),
        ],
        out_specs=(
            pl.BlockSpec(memory_space=pltpu.VMEM),
            pl.BlockSpec(memory_space=pltpu.VMEM),
        ),
        scratch_shapes=[
            pltpu.VMEM((comps, nx, ne, ny, nd), jnp.float32),
            pltpu.VMEM((comps, nx + 2, ne, ny, nd), jnp.float32),
            pltpu.VMEM((nx, ny, nd), jnp.float32),
            pltpu.VMEM((2 * reach + 1, 4, comps * nx * ny), jnp.float32),
            pltpu.VMEM((comps, nx, ny, ne * nd), jnp.float32),
            pltpu.VMEM((nx, ny, nd), jnp.float32),
            pltpu.VMEM((n_mom, 1, nd), jnp.float32),
            pltpu.VMEM((n_mom, 1, nd), jnp.float32),
            pltpu.VMEM((2, ne, ny, nd), jnp.float32),
            pltpu.VMEM((2, ne, ny, nd), jnp.float32),
            pltpu.SemaphoreType.DMA((comps,)),
            pltpu.SemaphoreType.DMA((2,)),
            pltpu.SemaphoreType.DMA((2,)),
            pltpu.SemaphoreType.DMA((2 * reach + 1,)),
            pltpu.SemaphoreType.DMA((2 * reach + 1,)),
            pltpu.SemaphoreType.DMA((n_mom,)),
            pltpu.SemaphoreType.DMA((n_mom,)),
        ],
        compiler_params=pltpu.CompilerParams(collective_id=0, has_side_effects=True),
        name="section",
    )(by_energy, jnp.transpose(cutoff), phonon_shift, phonon_rates)
    return jnp.transpose(sectioned, (0, 1, 3, 2, 4)), density.reshape(ny)


def solution(mesh):
    return jax.shard_map(
        functools.partial(on_device, mesh.shape["space"], mesh.shape["mom"]),
        mesh=mesh,
        in_specs=(P(None, "space", None, "mom", None), P("space", None), P(), P()),
        out_specs=(P(None, "space", None, "mom", None), P(("space", "mom"))),
        check_vma=False,
    )
```
